32 devices in a mesh: dom: 8 (over z, y), mp: 4 (over x, core).
Axes of the slice: x: 2, y: 2, z: 4, core: 2. Of those that a mesh axis runs over, the one named last changes fastest.
Arguments:
- vertex_embedding: bfloat16 [4096, 512], P('dom'), may hold values from -6 to 6
- prenorm_mixer_scale: float32 [512], replicated, may hold values from 0.25 to 1.75
- prenorm_perceptron_scale: float32 [512], replicated, may hold values from 0.25 to 1.75
- triple_projector_stack: bfloat16 [3, 512, 512], P(None, None, 'mp'), may hold values from -0.25 to 0.25
- channel_logit_scaling: float32 [8], P('mp'), may hold values from 0.06 to 8
- mixer_final_projector: bfloat16 [512, 512], P('mp'), may hold values from -0.25 to 0.25
- neighbour_mixer_projector: bfloat16 [512, 512], P('mp'), may hold values from -0.25 to 0.25
- expand_projector: bfloat16 [512, 2048], P(None, 'mp'), may hold values from -0.25 to 0.25
- contract_projector: bfloat16 [2048, 512], P('mp'), may hold values from -0.125 to 0.125
- matched_companion: int32 [2, 8], replicated, may hold values from 0 to 7, as said below
- boundary_sender_vertex: int32 [8, 8, 128], P('dom'), may hold values from 0 to 511
- boundary_slot_tally: int32 [8, 8], P('dom'), may hold values from 0 to 128, as said below
- boundary_landing_vertex: int32 [8, 8, 128], P('dom'), may hold values from 0 to 511
- partition_edge_tail: int32 [8, 16384], P('dom'), may hold values from 0 to 511
- partition_edge_sink: int32 [8, 16384], P('dom'), may hold values from 0 to 511
Outputs:
- updated: bfloat16 [4096, 512], P(('dom', 'mp'))
The draws below stay inside these ranges and needn't reach their ends.
Inputs may be any that keep to these rules, and one draw needn't show every extreme that they name: matched_companion[j, b] equals b XOR c_j for one number c_j of each matching; c_0 and c_1 are at least 1 and differ. Slots at and beyond boundary_slot_tally[s, d] of the 128 slots from s to d are unused; the diagonal is 0; the largest entry is 128.
All inputs are finite; a program needn't handle non-finite values.
Results may differ from the reference program's by a relative error of at most 0.012.
The reference program's roundings to bfloat16 on the way count: a program that leaves them out, or rounds other values in their place, can miss the bound.
Values may be sent and summed in bfloat16 or wider, within the bound.
No kernel may reach another device: no remote copies, remote signals or barrier semaphores. Data moves between devices by JAX's collectives and lax.ppermute only.
A program may use at most 64 MiB of HBM per device.

```python
import jax
import jax.numpy as jnp
from jax import lax

D = 512
HEADS = 8
HEAD_SIZE = 64
FF = 2048
BLOCK_NODES = 512
CAP = 128
NBD = 1
E_LOC = 16384
NODES = 4096
N_DOM = 8


def draw_matched_companion(key, part):
    block_total = NBD * N_DOM
    first_key, second_key = jax.random.split(jax.random.fold_in(key, 11))
    first_mask = jax.random.randint(first_key, (), NBD, block_total, dtype=jnp.int32)
    second = jax.random.randint(second_key, (), NBD, block_total - 1, dtype=jnp.int32)
    second = second + (second >= first_mask).astype(jnp.int32)
    blocks = jnp.arange(block_total, dtype=jnp.int32)
    return jnp.stack([jnp.bitwise_xor(blocks, first_mask), jnp.bitwise_xor(blocks, second)])


def draw_boundary_slot_tally(key, part):
    level_key, count_key, pick_key, peer_key = jax.random.split(jax.random.fold_in(key, 23), 4)
    levels = jax.random.randint(level_key, (N_DOM, 1), 3, 5, dtype=jnp.int32)
    counts = jax.random.randint(count_key, (N_DOM, N_DOM), 0, CAP + 1, dtype=jnp.int32) * levels // 4
    sources = jnp.arange(N_DOM, dtype=jnp.int32)
    counts = jnp.where(sources[:, None] == sources[None, :], 0, counts)
    chosen = jax.random.randint(pick_key, (), 0, N_DOM, dtype=jnp.int32)
    peer_index = (chosen + 1 + jax.random.randint(peer_key, (), 0, N_DOM - 1, dtype=jnp.int32)) % N_DOM
    return counts.at[chosen, peer_index].set(CAP)


def draw_channel_logit_scaling(key, part):
    uniform_draw = jax.random.uniform(jax.random.fold_in(key, 37), (HEADS,), jnp.float32)
    fraction = uniform_draw
    lower, upper = (0.06, 0.3)
    return jnp.exp(jnp.log(lower) + fraction * (jnp.log(upper) - jnp.log(lower))).astype(jnp.float32)


def touch_ends(values, key, least, largest):
    extent = values.shape
    index_at = [jax.random.randint(jax.random.fold_in(key, axis), (), 0, extent[axis]) for axis in range(len(extent))]
    values = values.at[tuple(index_at)].set(least)
    longest = extent.index(max(extent))
    index_at[longest] = (index_at[longest] + 1) % extent[longest]
    return values.at[tuple(index_at)].set(largest)


def block_scale(rng, shape, pieces, least, top_value):
    gain = 1.0
    for dim, blocks in pieces:
        steps = jax.random.uniform(jax.random.fold_in(jax.random.fold_in(rng, 6), dim), (blocks,), jnp.float32, least / len(pieces), top_value / len(pieces))
        gain = gain * jnp.repeat(jnp.exp(steps), shape[dim] // blocks).reshape((-1,) + (1,) * (len(shape) - 1 - dim))
    return gain


def noise(stream_key, dims, spread, limit, cuts=(), kind=jnp.bfloat16):
    result = jax.random.normal(stream_key, dims, jnp.float32) * spread
    if len(cuts) > 0:
        result = block_scale(stream_key, dims, cuts, -0.22, 0.18) * result
    return jnp.clip(result, min=-limit, max=limit).astype(kind)


def setup_inputs(seed: int = 0) -> dict:
    keys = jax.random.split(jax.random.key(seed), 16)
    return {
        "vertex_embedding": noise(keys[0], (NODES, D), 1.0, 6.0, ((0, 8),)),
        "prenorm_mixer_scale": jnp.clip(1.0 + 0.15 * jax.random.normal(keys[1], (D,), jnp.float32), 0.25, 1.75),
        "prenorm_perceptron_scale": jnp.clip(1.0 + 0.15 * jax.random.normal(keys[2], (D,), jnp.float32), 0.25, 1.75),
        "triple_projector_stack": noise(keys[3], (3, D, D), D ** -0.5, 0.25, ((2, 4),)),
        "channel_logit_scaling": draw_channel_logit_scaling(jax.random.fold_in(keys[15], 71), 0),
        "mixer_final_projector": noise(keys[5], (D, D), D ** -0.5, 0.25, ((0, 4),)),
        "neighbour_mixer_projector": noise(keys[6], (D, D), D ** -0.5, 0.25, ((0, 4),)),
        "expand_projector": noise(keys[7], (D, FF), D ** -0.5, 0.25, ((1, 4),)),
        "contract_projector": noise(keys[8], (FF, D), FF ** -0.5, 0.125, ((0, 4),)),
        "matched_companion": draw_matched_companion(jax.random.fold_in(keys[15], 71), 0),
        "boundary_sender_vertex": touch_ends(jax.random.randint(keys[10], (N_DOM, N_DOM, CAP), 0, NBD * BLOCK_NODES), jax.random.fold_in(keys[10], 1), 0, (NBD * BLOCK_NODES) - 1).astype(jnp.int32),
        "boundary_slot_tally": draw_boundary_slot_tally(jax.random.fold_in(keys[15], 71), 0),
        "boundary_landing_vertex": touch_ends(jax.random.randint(keys[12], (N_DOM, N_DOM, CAP), 0, NBD * BLOCK_NODES), jax.random.fold_in(keys[12], 1), 0, (NBD * BLOCK_NODES) - 1).astype(jnp.int32),
        "partition_edge_tail": touch_ends(jax.random.randint(keys[13], (N_DOM, E_LOC), 0, NBD * BLOCK_NODES), jax.random.fold_in(keys[13], 1), 0, (NBD * BLOCK_NODES) - 1).astype(jnp.int32),
        "partition_edge_sink": touch_ends(jax.random.randint(keys[14], (N_DOM, E_LOC), 0, NBD * BLOCK_NODES), jax.random.fold_in(keys[14], 1), 0, (NBD * BLOCK_NODES) - 1).astype(jnp.int32),
    }


epsilon = 1e-05

def normalize(matrix, scale_gain):
    matrix = matrix.astype(jnp.float32)
    row_mean = lax.optimization_barrier(jnp.mean(matrix, -1, keepdims=True))
    centred = matrix - row_mean
    variance = lax.optimization_barrier(jnp.mean(centred * centred, -1, keepdims=True))
    return (centred * lax.rsqrt(variance + epsilon) * scale_gain).astype(jnp.bfloat16)

def tile_softmax_mixing(asking_vertices, lookup_tensor, content_tensor, channel_logit_scaling):
    affinity_table = jnp.einsum('rhd,shd->hrs', asking_vertices.astype(jnp.float32), lookup_tensor.astype(jnp.float32))
    affinity_table = affinity_table * channel_logit_scaling[:, None, None]
    weights = jax.nn.softmax(affinity_table, axis=-1).astype(jnp.bfloat16)
    attended = jnp.einsum('hrs,shd->rhd', weights.astype(jnp.float32), content_tensor.astype(jnp.float32))
    return attended.astype(jnp.bfloat16)

def reference(vertex_embedding, prenorm_mixer_scale, prenorm_perceptron_scale, triple_projector_stack, channel_logit_scaling, mixer_final_projector, neighbour_mixer_projector, expand_projector, contract_projector, matched_companion, boundary_sender_vertex, boundary_slot_tally, boundary_landing_vertex, partition_edge_tail, partition_edge_sink):
    node_dev = NBD * BLOCK_NODES
    block_total = NBD * N_DOM
    normed = normalize(vertex_embedding, prenorm_mixer_scale)
    asking_vertices = jnp.dot(normed, triple_projector_stack[0], preferred_element_type=jnp.float32).astype(jnp.bfloat16)
    lookup_tensor = jnp.dot(normed, triple_projector_stack[1], preferred_element_type=jnp.float32).astype(jnp.bfloat16)
    content_tensor = jnp.dot(normed, triple_projector_stack[2], preferred_element_type=jnp.float32).astype(jnp.bfloat16)
    asking_groups = asking_vertices.reshape(block_total, BLOCK_NODES, HEADS, HEAD_SIZE)
    key_blocks = lookup_tensor.reshape(block_total, BLOCK_NODES, HEADS, HEAD_SIZE)
    value_blocks = content_tensor.reshape(block_total, BLOCK_NODES, HEADS, HEAD_SIZE)

    def per_block(tile_offset):
        chosen = jnp.stack([tile_offset, matched_companion[0, tile_offset], matched_companion[1, tile_offset]]).astype(jnp.int32)
        partition_lookups = key_blocks[chosen].reshape(3 * BLOCK_NODES, HEADS, HEAD_SIZE)
        partition_contents = value_blocks[chosen].reshape(3 * BLOCK_NODES, HEADS, HEAD_SIZE)
        return tile_softmax_mixing(asking_groups[tile_offset], partition_lookups, partition_contents, channel_logit_scaling)
    attended = lax.map(per_block, jnp.arange(block_total, dtype=jnp.int32)).reshape(NODES, D)
    attn_term = jnp.dot(attended, mixer_final_projector, preferred_element_type=jnp.float32)

    def per_device(device):
        send_list = boundary_sender_vertex[:, device, :]
        live_slots = jnp.arange(CAP, dtype=jnp.int32)[None, :] < boundary_slot_tally[:, device][:, None]
        global_rows = jnp.arange(N_DOM, dtype=jnp.int32)[:, None] * node_dev + send_list
        sent_values = jnp.where(live_slots[..., None], vertex_embedding[global_rows].astype(jnp.float32), 0.0)
        targets = boundary_landing_vertex[device].reshape(-1)
        boundary = jax.ops.segment_sum(sent_values.reshape(-1, D), targets, num_segments=node_dev)
        degree = jax.ops.segment_sum(live_slots.reshape(-1).astype(jnp.float32), targets, num_segments=node_dev)
        own_block = lax.dynamic_slice_in_dim(vertex_embedding, device * node_dev, node_dev, 0)
        local_sum = jax.ops.segment_sum(own_block[partition_edge_tail[device]].astype(jnp.float32), partition_edge_sink[device], num_segments=node_dev)
        degree = degree + jax.ops.segment_sum(jnp.ones((E_LOC,), jnp.float32), partition_edge_sink[device], num_segments=node_dev)
        message = (own_block.astype(jnp.float32) + local_sum + boundary) / (1.0 + degree)[:, None]
        return message.astype(jnp.bfloat16)
    message = lax.map(per_device, jnp.arange(N_DOM, dtype=jnp.int32)).reshape(NODES, D)
    mixed_rows = vertex_embedding.astype(jnp.float32) + attn_term + jnp.dot(message, neighbour_mixer_projector, preferred_element_type=jnp.float32)
    normed_mlp = normalize(mixed_rows, prenorm_perceptron_scale)
    hidden = jax.nn.gelu(jnp.dot(normed_mlp, expand_projector, preferred_element_type=jnp.float32), approximate=False).astype(jnp.bfloat16)
    return (mixed_rows + jnp.dot(hidden, contract_projector, preferred_element_type=jnp.float32)).astype(jnp.bfloat16)
```

```python
import functools
import math

import jax
import jax.numpy as jnp
from jax import lax
from jax.experimental import pallas as pl
from jax.experimental.pallas import tpu as pltpu
from jax.sharding import PartitionSpec as P


HEAD_SIZE = 64
EPSILON = 1e-05
FLAG_ROWS = 8
EDGE_STEP = 1024

f32 = jnp.float32
bf16 = jnp.bfloat16
f8 = jnp.float8_e4m3fn

VMEM = pl.BlockSpec(memory_space=pltpu.VMEM)
SMEM = pl.BlockSpec(memory_space=pltpu.SMEM)

NT = (((1,), (1,)), ((), ()))
NN = (((1,), (0,)), ((), ()))

PARAMS = pltpu.CompilerParams(vmem_limit_bytes=24 << 20)


def dot(a, b, dims=NN):
    return lax.dot_general(a, b, dims, preferred_element_type=f32)


def norm_rows(rows, gain):
    mean = jnp.mean(rows, -1, keepdims=True)
    centred = rows - mean
    variance = jnp.mean(centred * centred, -1, keepdims=True)
    return (centred * lax.rsqrt(variance + EPSILON) * gain).astype(bf16)


def one_hot_columns(index_row, count, live=None):
    hit = lax.broadcasted_iota(jnp.int32, (count, index_row.shape[1]), 0) == index_row
    if live is not None:
        hit = jnp.logical_and(hit, live)
    return jnp.where(hit, 1.0, 0.0).astype(bf16)


def narrow_one_hot(index_row, count):
    numbers = lax.broadcasted_iota(jnp.int16, (count, index_row.shape[1]), 0)
    hit = numbers == index_row.astype(jnp.int16)
    return jnp.where(hit, jnp.ones((), bf16), jnp.zeros((), bf16)).astype(f8)


def xor_route(count, mask):
    return [(i, i ^ mask) for i in range(count)]


def prologue_kernel(
    place_ref, tally_ref, companion_ref, x_ref, gain_ref, w_ref, sender_ref,
    choice_ref, q_ref, kv_ref, k_ref, v_ref, *out_refs,
):
    one, two = companion_ref[0, 0], companion_ref[1, 0]
    low, high = jnp.minimum(one, two), jnp.maximum(one, two)
    choice_ref[0] = low
    choice_ref[1] = high
    choice_ref[2] = lax.shift_right_logical((high - 1) * (high - 2), 1) + low - 1
    nodes, _ = x_ref.shape
    cols = q_ref.shape[1]
    normed = norm_rows(x_ref[...].astype(f32), gain_ref[...])
    weights = jnp.concatenate([w_ref[0], w_ref[1], w_ref[2]], axis=1)
    projected = dot(normed, weights).astype(bf16)
    q_ref[...] = projected[:, :cols]
    kv_ref[...] = projected[:, cols:]
    k_ref[...] = projected[:, cols : 2 * cols]
    v_ref[...] = projected[:, 2 * cols :]
    me, part = place_ref[0], place_ref[1]
    quarter = x_ref[:, pl.ds(pl.multiple_of(part * cols, 128), cols)]
    quarter_t = quarter.astype(f32).T.astype(bf16)
    cap = sender_ref.shape[1]
    slot = lax.broadcasted_iota(jnp.int32, (1, cap), 1)
    near = len(out_refs)
    for a, out_ref in enumerate(out_refs):
        for h in range(out_ref.shape[0]):
            dest = jnp.bitwise_xor(me, h * near + a)
            live = slot < tally_ref[0, dest]
            pick = one_hot_columns(sender_ref[pl.ds(dest, 1), :], nodes, live)
            out_ref[h, :cols, :] = dot(quarter_t, pick).astype(bf16)
            out_ref[h, cols:, :] = jnp.broadcast_to(
                jnp.where(live, 1.0, 0.0), (FLAG_ROWS, cap)
            ).astype(bf16)


def prologue(place, tally, companion, x, gain, w, sender, near):
    nodes, width = x.shape
    cols = w.shape[2]
    peers, cap = sender.shape
    far = peers // near
    return pl.pallas_call(
        prologue_kernel,
        out_shape=[
            jax.ShapeDtypeStruct((3,), jnp.int32),
            jax.ShapeDtypeStruct((nodes, cols), bf16),
            jax.ShapeDtypeStruct((nodes, 2 * cols), bf16),
            jax.ShapeDtypeStruct((nodes, cols), bf16),
            jax.ShapeDtypeStruct((nodes, cols), bf16),
        ]
        + [jax.ShapeDtypeStruct((far, cols + FLAG_ROWS, cap), bf16)] * near,
        in_specs=[SMEM] * 3 + [VMEM] * 4,
        out_specs=[SMEM] + [VMEM] * (near + 4),
        name="prologue",
        compiler_params=PARAMS,
        cost_estimate=pl.CostEstimate(
            flops=2 * nodes * width * 3 * cols, bytes_accessed=4 << 20, transcendentals=0
        ),
    )(place, tally, companion, x, gain, w, sender)


def edge_kernel(tail_ref, sink_ref, counts_ref):
    nodes = counts_ref.shape[0]
    edges = tail_ref.shape[1]
    step = math.gcd(edges, EDGE_STEP)
    counts_ref[...] = jnp.zeros_like(counts_ref)

    def add(turn, unused):
        at = pl.ds(pl.multiple_of(turn * step, step), step)
        sink = narrow_one_hot(sink_ref[:, at], nodes)
        tail = narrow_one_hot(tail_ref[:, at], nodes)
        counts_ref[...] += dot(sink, tail, NT)
        return unused

    lax.fori_loop(0, edges // step, add, 0)


def edge_counts(tail, sink, nodes):
    edges = tail.shape[1]
    return pl.pallas_call(
        edge_kernel,
        out_shape=jax.ShapeDtypeStruct((nodes, nodes), f32),
        in_specs=[VMEM, VMEM],
        out_specs=VMEM,
        name="edge_counts",
        compiler_params=PARAMS,
        cost_estimate=pl.CostEstimate(
            flops=2 * nodes * nodes * edges, bytes_accessed=2 << 20, transcendentals=0
        ),
    )(tail, sink)


def message_kernel(origins, place_ref, counts_ref, x_ref, landing_ref, *refs):
    count = len(set(i for i, _, _ in origins))
    ins, outs = refs[:count], refs[count:]
    me, part = place_ref[0], place_ref[1]
    nodes = x_ref.shape[0]
    rows, cols = outs[0].shape
    land = jnp.concatenate(
        [
            one_hot_columns(landing_ref[pl.ds(jnp.bitwise_xor(me, k), 1), :], nodes)
            for _, _, k in origins
        ],
        axis=1,
    )
    arrived = jnp.concatenate([ins[i][j] for i, j, _ in origins], axis=1)
    boundary = dot(land, arrived, NT)
    quarter = x_ref[:, pl.ds(pl.multiple_of(part * cols, 128), cols)]
    filled = jnp.concatenate([quarter, jnp.ones((nodes, 128), bf16)], axis=1)
    counts = counts_ref[...]
    high = jnp.floor(counts * (1.0 / 256.0))
    low = counts - 256.0 * high
    total = 256.0 * dot(high.astype(bf16), filled) + dot(low.astype(bf16), filled)
    quarter = quarter.astype(f32)
    degree = total[:, cols : cols + 1] + boundary[:, cols : cols + 1]
    message = (quarter + total[:, :cols] + boundary[:, :cols]) / (1.0 + degree)
    whole_ref = outs[-1]
    whole_ref[...] = message.astype(bf16)
    for k, out_ref in enumerate(outs[:-1]):
        at = jnp.bitwise_xor(part, k) * rows
        out_ref[...] = whole_ref[pl.ds(pl.multiple_of(at, rows), rows), :]


def messages(place, counts, x, landing, arrived, origins, cols, shares):
    nodes = x.shape[0]
    rows = nodes // shares
    return pl.pallas_call(
        functools.partial(message_kernel, origins),
        out_shape=[jax.ShapeDtypeStruct((rows, cols), bf16)] * shares,
        in_specs=[SMEM] + [VMEM] * (3 + len(arrived)),
        out_specs=[VMEM] * shares,
        scratch_shapes=[pltpu.VMEM((nodes, cols), bf16)],
        name="messages",
        compiler_params=PARAMS,
        cost_estimate=pl.CostEstimate(
            flops=2 * nodes * 1024 * 256, bytes_accessed=2 << 20, transcendentals=0
        ),
    )(place, counts, x, landing, *arrived)


def attention_kernel(place_ref, scale_ref, q_ref, own_ref, one_ref, two_ref, *outs):
    part = place_ref[1]
    rows, cols = outs[0].shape
    heads = cols // HEAD_SIZE
    for k, out_ref in enumerate(outs):
        at = pl.multiple_of(jnp.bitwise_xor(part, k) * rows, rows)
        for h in range(heads):
            band = slice(h * HEAD_SIZE, (h + 1) * HEAD_SIZE)
            value_band = slice(cols + h * HEAD_SIZE, cols + (h + 1) * HEAD_SIZE)
            q = q_ref[pl.ds(at, rows), band]
            scores = [
                dot(q, r[:, band], NT) * scale_ref[h] for r in (own_ref, one_ref, two_ref)
            ]
            top = functools.reduce(
                jnp.maximum, [jnp.max(s, -1, keepdims=True) for s in scores]
            )
            powers = [jnp.exp(s - top) for s in scores]
            total = sum(jnp.sum(p, -1, keepdims=True) for p in powers)
            inverse = 1.0 / total
            attended = sum(
                dot((p * inverse).astype(bf16), r[:, value_band])
                for p, r in zip(powers, (own_ref, one_ref, two_ref))
            )
            out_ref[:, band] = attended.astype(bf16)


def attention(place, scale, q, own, one, two, shares):
    nodes, cols = q.shape
    rows = nodes // shares
    return pl.pallas_call(
        attention_kernel,
        out_shape=[jax.ShapeDtypeStruct((rows, cols), bf16)] * shares,
        in_specs=[SMEM, SMEM] + [VMEM] * 4,
        out_specs=[VMEM] * shares,
        name="attention",
        compiler_params=PARAMS,
        cost_estimate=pl.CostEstimate(
            flops=4 * nodes * 3 * nodes * 256, bytes_accessed=2 << 20, transcendentals=2 << 20
        ),
    )(place, scale, q, own, one, two)


def final_kernel(shares, place_ref, x_ref, gain_ref, *refs):
    att, msg, wo, wn, up, down = (refs[i * shares : (i + 1) * shares] for i in range(6))
    out_ref = refs[6 * shares]
    rows = out_ref.shape[0]
    part = place_ref[1]
    mixed = x_ref[pl.ds(pl.multiple_of(part * rows, rows), rows), :].astype(f32)
    terms = jnp.concatenate([r[...] for r in (*att, *msg)], axis=1)
    mixed = mixed + dot(terms, jnp.concatenate([r[...] for r in (*wo, *wn)], axis=0))
    normed = norm_rows(mixed, gain_ref[...])
    total = mixed
    for k in range(shares):
        wide = dot(normed, up[k][...])
        hidden = (0.5 * wide * (1.0 + lax.erf(wide * (0.5**0.5)))).astype(bf16)
        total = total + dot(hidden, down[k][...])
    out_ref[...] = total.astype(bf16)


def final(place, x, gain, att, msg, wo, wn, up, down):
    shares = len(att)
    rows = x.shape[0] // shares
    width = x.shape[1]
    return pl.pallas_call(
        functools.partial(final_kernel, shares),
        out_shape=jax.ShapeDtypeStruct((rows, width), bf16),
        in_specs=[SMEM] + [VMEM] * (2 + 6 * shares),
        out_specs=VMEM,
        name="final",
        compiler_params=PARAMS,
        cost_estimate=pl.CostEstimate(
            flops=2 * rows * width * 4096, bytes_accessed=6 << 20, transcendentals=1 << 18
        ),
    )(place, x, gain, *att, *msg, *wo, *wn, *up, *down)


def gather_pieces(piece, axis):
    count = lax.axis_size(axis)
    pieces = {0: piece}
    bit = count // 2
    while bit:
        for k in list(pieces):
            pieces[k | bit] = lax.ppermute(pieces[k], axis, xor_route(count, bit))
        bit //= 2
    return [pieces[k] for k in range(count)]


def swap_chunks(chunks, axis):
    count = lax.axis_size(axis)
    return [chunks[0]] + [
        lax.ppermute(chunks[k], axis, xor_route(count, k)) for k in range(1, count)
    ]


def layer(
    x,
    mixer_gain,
    perceptron_gain,
    projectors,
    scale,
    out_projector,
    neighbour_projector,
    expand,
    contract,
    companion,
    sender,
    tally,
    landing,
    tail,
    sink,
):
    peers = lax.axis_size("dom")
    shares = lax.axis_size("mp")
    cols = projectors.shape[2]
    place = jnp.stack([lax.axis_index("dom"), lax.axis_index("mp")]).astype(jnp.int32)

    up = gather_pieces(expand, "mp")
    down = gather_pieces(contract, "mp")
    wo = gather_pieces(out_projector, "mp")
    wn = gather_pieces(neighbour_projector, "mp")

    near = 1 << ((peers.bit_length() - 1) // 2)
    far = peers // near
    choice, q, kv, k, v, *outgoing = prologue(
        place, tally, companion, x, mixer_gain[None, :], projectors, sender[0], near
    )

    def shared(outgoing, tail, sink):
        counts = edge_counts(tail, sink, x.shape[0])
        held = [outgoing[0]] + [
            lax.ppermute(outgoing[a], "dom", xor_route(peers, a)) for a in range(1, near)
        ]
        arrived = [
            lax.ppermute(
                jnp.stack([block[h] for block in held]), "dom", xor_route(peers, h * near)
            )
            for h in range(1, far)
        ]
        return counts, held[1:] + arrived

    origins = tuple((a - 1, 0, a) for a in range(1, near)) + tuple(
        (near - 2 + h, a, h * near + a) for h in range(1, far) for a in range(near)
    )

    def send(block, mask):
        return lax.ppermute(block, "dom", xor_route(peers, mask))

    operands = (kv, k, v, outgoing, tail, sink)
    if peers * (peers - 1) // 2 <= 32:
        branches = []
        for high in range(1, peers):
            for low in range(1, high):

                def branch(kv, k, v, *rest, low=low, high=high):
                    if low & high & (peers // 2):
                        one_k, one_v = send(k, low), send(v, low)
                        two_k, two_v = send(one_k, low ^ high), send(one_v, low ^ high)
                        one = jnp.concatenate([one_k, one_v], axis=1)
                        two = jnp.concatenate([two_k, two_v], axis=1)
                    else:
                        one, two = send(kv, low), send(kv, high)
                    return (one, two) + shared(*rest)

                branches.append(branch)
        one, two, counts, arrived = lax.switch(choice[2], branches, *operands)
    else:
        hops = [lambda kv, mask=mask: send(kv, mask) for mask in range(1, peers)]
        one = lax.switch(choice[0] - 1, hops, kv)
        two = lax.switch(choice[1] - 1, hops, kv)
        counts, arrived = shared(outgoing, tail, sink)

    msg = messages(place, counts, x, landing[0], arrived, origins, cols, shares)
    msg = swap_chunks(msg, "mp")
    att = attention(place, scale, q, kv, one, two, shares)
    att = swap_chunks(att, "mp")
    return final(place, x, perceptron_gain[None, :], att, msg, wo, wn, up, down)


def solution(mesh):
    return jax.shard_map(
        layer,
        mesh=mesh,
        in_specs=(
            P("dom", None),
            P(),
            P(),
            P(None, None, "mp"),
            P("mp"),
            P("mp", None),
            P("mp", None),
            P(None, "mp"),
            P("mp", None),
            P(),
            P("dom", None, None),
            P("dom", None),
            P("dom", None, None),
            P("dom", None),
            P("dom", None),
        ),
        out_specs=P(("dom", "mp"), None),
        check_vma=False,
    )
```

```python
import functools
import math

import jax
import jax.numpy as jnp
from jax import lax
from jax.experimental import pallas as pl
from jax.experimental.pallas import tpu as pltpu
from jax.sharding import PartitionSpec as P


HEAD_SIZE = 64
EPSILON = 1e-05
FLAG_ROWS = 8
EDGE_STEP = 1024

f32 = jnp.float32
bf16 = jnp.bfloat16
f8 = jnp.float8_e4m3fn

VMEM = pl.BlockSpec(memory_space=pltpu.VMEM)
SMEM = pl.BlockSpec(memory_space=pltpu.SMEM)
HBM = pl.BlockSpec(memory_space=pltpu.HBM)

NT = (((1,), (1,)), ((), ()))
NN = (((1,), (0,)), ((), ()))

PARAMS = pltpu.CompilerParams(vmem_limit_bytes=24 << 20)


def dot(a, b, dims=NN):
    return lax.dot_general(a, b, dims, preferred_element_type=f32)


def norm_rows(rows, gain):
    mean = jnp.mean(rows, -1, keepdims=True)
    centred = rows - mean
    variance = jnp.mean(centred * centred, -1, keepdims=True)
    return (centred * lax.rsqrt(variance + EPSILON) * gain).astype(bf16)


def one_hot_columns(index_row, count, live=None):
    hit = lax.broadcasted_iota(jnp.int32, (count, index_row.shape[1]), 0) == index_row
    if live is not None:
        hit = jnp.logical_and(hit, live)
    return jnp.where(hit, 1.0, 0.0).astype(bf16)


def narrow_one_hot(index_row, count):
    numbers = lax.broadcasted_iota(jnp.int16, (count, index_row.shape[1]), 0)
    hit = numbers == index_row.astype(jnp.int16)
    return jnp.where(hit, jnp.ones((), bf16), jnp.zeros((), bf16)).astype(f8)


def in_hbm(*arrays):
    return [pltpu.with_memory_space_constraint(array, pltpu.HBM) for array in arrays]


def xor_route(count, mask):
    return [(i, i ^ mask) for i in range(count)]


def prologue_kernel(
    x_hbm, gain_hbm, w_hbm, sender_hbm, wo_hbm, wn_hbm, late_gain_hbm, landing_hbm,
    tally_hbm, companion_hbm, scale_hbm,
    low_ref, high_ref, pair_ref, q_ref, kv_ref, k_ref, v_ref, mix_ref, scales_ref, quarter_ref,
    share_ref, late_gain_ref, landing_ref, *rest,
):
    out_refs = rest[:-8]
    x_ref, gain_ref, w_ref, sender_ref, tally_ref, companion_ref, scale_ref, sems = rest[-8:]
    nodes, _ = x_ref.shape
    cols = q_ref.shape[1]
    sources = (
        (x_hbm, x_ref),
        (gain_hbm, gain_ref),
        (w_hbm, w_ref),
        (sender_hbm, sender_ref),
        (wo_hbm, mix_ref.at[pl.ds(0, cols)]),
        (wn_hbm, mix_ref.at[pl.ds(cols, cols)]),
        (late_gain_hbm, late_gain_ref),
        (landing_hbm, landing_ref),
        (tally_hbm, tally_ref),
        (companion_hbm, companion_ref),
        (scale_hbm, scale_ref),
    )
    copies = [
        pltpu.make_async_copy(source, target, sems.at[i])
        for i, (source, target) in enumerate(sources)
    ]
    for copy in copies:
        copy.start()

    copies[0].wait()
    copies[1].wait()
    normed = norm_rows(x_ref[...].astype(f32), gain_ref[...])
    copies[2].wait()
    weights = jnp.concatenate([w_ref[0], w_ref[1], w_ref[2]], axis=1)
    projected = dot(normed, weights).astype(bf16)
    q_ref[...] = projected[:, :cols]
    kv_ref[...] = projected[:, cols:]
    k_ref[...] = projected[:, cols : 2 * cols]
    v_ref[...] = projected[:, 2 * cols :]

    for copy in copies[3:]:
        copy.wait()
    one, two = companion_ref[0, 0], companion_ref[1, 0]
    low, high = jnp.minimum(one, two), jnp.maximum(one, two)
    low_ref[0] = low - 1
    high_ref[0] = high - 1
    pair_ref[0] = lax.shift_right_logical((high - 1) * (high - 2), 1) + low - 1
    for h in range(scales_ref.shape[0]):
        scales_ref[h] = jnp.full(scales_ref.shape[1:], scale_ref[h], f32)

    me, part = lax.axis_index("dom"), lax.axis_index("mp")
    rows = share_ref.shape[0]
    share_ref[...] = x_ref[pl.ds(pl.multiple_of(part * rows, rows), rows), :]
    quarter = x_ref[:, pl.ds(pl.multiple_of(part * cols, 128), cols)]
    quarter_ref[...] = quarter
    quarter_t = quarter.astype(f32).T.astype(bf16)
    cap = sender_ref.shape[1]
    slot = lax.broadcasted_iota(jnp.int32, (1, cap), 1)
    near = len(out_refs)
    for a, out_ref in enumerate(out_refs):
        for h in range(out_ref.shape[0]):
            dest = jnp.bitwise_xor(me, h * near + a)
            live = slot < tally_ref[0, dest]
            pick = one_hot_columns(sender_ref[pl.ds(dest, 1), :], nodes, live)
            out_ref[h, :cols, :] = dot(quarter_t, pick).astype(bf16)
            out_ref[h, cols:, :] = jnp.broadcast_to(
                jnp.where(live, 1.0, 0.0), (FLAG_ROWS, cap)
            ).astype(bf16)


def prologue(
    tally, companion, scale, x, gain, w, sender, wo, wn, late_gain, landing, near, shares
):
    nodes, width = x.shape
    cols = w.shape[2]
    peers, cap = sender.shape
    return pl.pallas_call(
        prologue_kernel,
        out_shape=[jax.ShapeDtypeStruct((1,), jnp.int32)] * 3
        + [jax.ShapeDtypeStruct((nodes, n * cols), bf16) for n in (1, 2, 1, 1)]
        + [
            jax.ShapeDtypeStruct((2 * cols, width), bf16),
            jax.ShapeDtypeStruct((scale.shape[0], 8, 128), f32),
            jax.ShapeDtypeStruct((nodes, cols), bf16),
            jax.ShapeDtypeStruct((nodes // shares, width), bf16),
            jax.ShapeDtypeStruct(late_gain.shape, f32),
            jax.ShapeDtypeStruct(landing.shape, jnp.int32),
        ]
        + [jax.ShapeDtypeStruct((peers // near, cols + FLAG_ROWS, cap), bf16)] * near,
        in_specs=[HBM] * 11,
        out_specs=[SMEM] * 3 + [VMEM] * (10 + near),
        scratch_shapes=[
            pltpu.VMEM(x.shape, bf16),
            pltpu.VMEM(gain.shape, f32),
            pltpu.VMEM(w.shape, bf16),
            pltpu.VMEM(sender.shape, jnp.int32),
            pltpu.SMEM(tally.shape, jnp.int32),
            pltpu.SMEM(companion.shape, jnp.int32),
            pltpu.SMEM(scale.shape, f32),
            pltpu.SemaphoreType.DMA((11,)),
        ],
        name="prologue",
        compiler_params=PARAMS,
        cost_estimate=pl.CostEstimate(
            flops=2 * nodes * width * 3 * cols, bytes_accessed=4 << 20, transcendentals=0
        ),
    )(
        *in_hbm(
            x, gain, w, sender, wo, wn, late_gain, landing, tally, companion, scale
        )
    )


def pack_kernel(*refs):
    near = refs[-1].shape[0]
    for h, out_ref in enumerate(refs[near:], start=1):
        for a in range(near):
            out_ref[a] = refs[a][h]


def pack(held):
    far, *block = held[0].shape
    return pl.pallas_call(
        pack_kernel,
        out_shape=[jax.ShapeDtypeStruct((len(held), *block), bf16)] * (far - 1),
        in_specs=[VMEM] * len(held),
        out_specs=[VMEM] * (far - 1),
        name="pack",
        compiler_params=PARAMS,
        cost_estimate=pl.CostEstimate(flops=0, bytes_accessed=1 << 20, transcendentals=0),
    )(*held)


def edge_kernel(start, tail_hbm, sink_hbm, *refs):
    before, (counts_ref, tail_ref, sink_ref, sems) = refs[:-4], refs[-4:]
    edges = tail_ref.shape[1]
    copies = [
        pltpu.make_async_copy(tail_hbm.at[:, pl.ds(start, edges)], tail_ref, sems.at[0]),
        pltpu.make_async_copy(sink_hbm.at[:, pl.ds(start, edges)], sink_ref, sems.at[1]),
    ]
    for copy in copies:
        copy.start()
    nodes = counts_ref.shape[0]
    step = math.gcd(edges, EDGE_STEP)
    counts_ref[...] = before[0][...] if before else jnp.zeros_like(counts_ref)
    for copy in copies:
        copy.wait()

    def add(turn, unused):
        at = pl.ds(pl.multiple_of(turn * step, step), step)
        sink = narrow_one_hot(sink_ref[:, at], nodes)
        tail = narrow_one_hot(tail_ref[:, at], nodes)
        counts_ref[...] += dot(sink, tail, NT)
        return unused

    lax.fori_loop(0, edges // step, add, 0)


def edge_counts(tail, sink, nodes, start, stop, *before):
    edges = stop - start
    return pl.pallas_call(
        functools.partial(edge_kernel, start),
        out_shape=jax.ShapeDtypeStruct((nodes, nodes), f32),
        in_specs=[HBM, HBM] + [VMEM] * len(before),
        out_specs=VMEM,
        scratch_shapes=[
            pltpu.VMEM((1, edges), jnp.int32),
            pltpu.VMEM((1, edges), jnp.int32),
            pltpu.SemaphoreType.DMA((2,)),
        ],
        name="edge_counts",
        compiler_params=PARAMS,
        cost_estimate=pl.CostEstimate(
            flops=2 * nodes * nodes * edges, bytes_accessed=2 << 20, transcendentals=0
        ),
    )(*in_hbm(tail, sink), *before)


def message_kernel(origins, counts_ref, quarter_ref, landing_ref, *refs):
    count = len(set(i for i, _, _ in origins))
    ins, outs = refs[:count], refs[count:]
    me, part = lax.axis_index("dom"), lax.axis_index("mp")
    nodes = quarter_ref.shape[0]
    rows, cols = outs[0].shape
    land = jnp.concatenate(
        [
            one_hot_columns(landing_ref[pl.ds(jnp.bitwise_xor(me, k), 1), :], nodes)
            for _, _, k in origins
        ],
        axis=1,
    )
    arrived = jnp.concatenate([ins[i][j] for i, j, _ in origins], axis=1)
    boundary = dot(land, arrived, NT)
    quarter = quarter_ref[...]
    filled = jnp.concatenate([quarter, jnp.ones((nodes, 128), bf16)], axis=1)
    counts = counts_ref[...]
    high = jnp.floor(counts * (1.0 / 256.0))
    low = counts - 256.0 * high
    total = 256.0 * dot(high.astype(bf16), filled) + dot(low.astype(bf16), filled)
    quarter = quarter.astype(f32)
    degree = total[:, cols : cols + 1] + boundary[:, cols : cols + 1]
    message = (quarter + total[:, :cols] + boundary[:, :cols]) / (1.0 + degree)
    whole_ref = outs[-1]
    whole_ref[...] = message.astype(bf16)
    for k, out_ref in enumerate(outs[:-1]):
        at = jnp.bitwise_xor(part, k) * rows
        out_ref[...] = whole_ref[pl.ds(pl.multiple_of(at, rows), rows), :]


def messages(counts, quarter, landing, arrived, origins, shares):
    nodes, cols = quarter.shape
    rows = nodes // shares
    return pl.pallas_call(
        functools.partial(message_kernel, origins),
        out_shape=[jax.ShapeDtypeStruct((rows, cols), bf16)] * shares,
        in_specs=[VMEM] * (3 + len(arrived)),
        out_specs=[VMEM] * shares,
        scratch_shapes=[pltpu.VMEM((nodes, cols), bf16)],
        name="messages",
        compiler_params=PARAMS,
        cost_estimate=pl.CostEstimate(
            flops=2 * nodes * 1024 * 256, bytes_accessed=2 << 20, transcendentals=0
        ),
    )(counts, quarter, landing, *arrived)


def attention_kernel(
    offsets, scales_ref, q_ref, own_ref, one_any, two_any, *refs
):
    outs, (one_ref, two_ref, block_ref, sems) = refs[:-4], refs[-4:]
    copies = [
        pltpu.make_async_copy(one_any, one_ref, sems.at[0]),
        pltpu.make_async_copy(two_any, two_ref, sems.at[1]),
    ]
    for copy in copies:
        copy.start()
    part = lax.axis_index("mp")
    rows, cols = outs[0].shape
    heads = cols // HEAD_SIZE
    count = len(offsets)
    base = jnp.bitwise_xor(part, offsets[0]) // count * count
    at = pl.multiple_of(base * rows, count * rows)
    sources = (own_ref, one_ref, two_ref)
    for h in range(heads):
        band = slice(h * HEAD_SIZE, (h + 1) * HEAD_SIZE)
        q = q_ref[pl.ds(at, count * rows), band]
        factor = scales_ref[h, :1, :1] * math.log2(math.e)
        parts = []
        for i, r in enumerate(sources):
            if h == 0 and i > 0:
                copies[i - 1].wait()
            parts.append(dot(q, r[:, band], NT) * factor)
        top = functools.reduce(jnp.maximum, [jnp.max(s, -1, keepdims=True) for s in parts])
        powers = [jnp.exp2(s - top) for s in parts]
        inverse = 1.0 / sum(jnp.sum(p, -1, keepdims=True) for p in powers)
        value_band = slice(cols + h * HEAD_SIZE, cols + (h + 1) * HEAD_SIZE)
        attended = sum(
            dot((p * inverse).astype(bf16), r[:, value_band]) for p, r in zip(powers, sources)
        )
        block_ref[:, band] = attended.astype(bf16)
    for k, out_ref in zip(offsets, outs):
        place = (jnp.bitwise_xor(part, k) - base) * rows
        out_ref[...] = block_ref[pl.ds(pl.multiple_of(place, rows), rows), :]


def attention(scales, q, own, one, two, shares, offsets):
    nodes, cols = q.shape
    rows = nodes // shares
    any_space = pl.BlockSpec(memory_space=pl.ANY)
    return pl.pallas_call(
        functools.partial(attention_kernel, offsets),
        out_shape=[jax.ShapeDtypeStruct((rows, cols), bf16)] * len(offsets),
        in_specs=[VMEM] * 3 + [any_space] * 2,
        out_specs=[VMEM] * len(offsets),
        scratch_shapes=[
            pltpu.VMEM(one.shape, bf16),
            pltpu.VMEM(two.shape, bf16),
            pltpu.VMEM((len(offsets) * rows, cols), bf16),
            pltpu.SemaphoreType.DMA((2,)),
        ],
        name="attention",
        compiler_params=PARAMS,
        cost_estimate=pl.CostEstimate(
            flops=4 * rows * len(offsets) * 3 * nodes * 256,
            bytes_accessed=2 << 20,
            transcendentals=1 << 20,
        ),
    )(scales, q, own, one, two)


def final_kernel(shares, share_ref, gain_ref, *refs):
    att, msg, mixes, ups, downs = (refs[i * shares : (i + 1) * shares] for i in range(5))
    out_ref, mix_buf, up_buf, down_buf, sems = refs[5 * shares :]
    _, width = out_ref.shape
    copies = []
    for i, (sources, buf) in enumerate(((mixes, mix_buf), (ups, up_buf), (downs, down_buf))):
        copies.append(
            [
                pltpu.make_async_copy(source, buf.at[k], sems.at[i, k])
                for k, source in enumerate(sources)
            ]
        )
    for copy in copies[0]:
        copy.start()
    for k in range(shares):
        copies[1][k].start()
        copies[2][k].start()
    mixed = share_ref[...].astype(f32)
    terms = jnp.concatenate([r[...] for pair in zip(att, msg) for r in pair], axis=1)
    for copy in copies[0]:
        copy.wait()
    mixed = mixed + dot(terms, mix_buf[...].reshape(-1, width))
    normed = norm_rows(mixed, gain_ref[...])
    total = mixed
    for k in range(shares):
        copies[1][k].wait()
        wide = dot(normed, up_buf[k])
        hidden = (0.5 * wide * (1.0 + lax.erf(wide * (0.5**0.5)))).astype(bf16)
        copies[2][k].wait()
        total = total + dot(hidden, down_buf[k])
    out_ref[...] = total.astype(bf16)


def final(share, gain, att, msg, mixes, ups, downs):
    shares = len(att)
    rows, width = share.shape
    any_space = pl.BlockSpec(memory_space=pl.ANY)
    return pl.pallas_call(
        functools.partial(final_kernel, shares),
        out_shape=jax.ShapeDtypeStruct((rows, width), bf16),
        in_specs=[VMEM] * (2 + 2 * shares) + [any_space] * (3 * shares),
        out_specs=VMEM,
        scratch_shapes=[
            pltpu.VMEM((shares, *group[0].shape), bf16) for group in (mixes, ups, downs)
        ]
        + [pltpu.SemaphoreType.DMA((3, shares))],
        name="final",
        compiler_params=PARAMS,
        cost_estimate=pl.CostEstimate(
            flops=2 * rows * width * 4096, bytes_accessed=6 << 20, transcendentals=1 << 18
        ),
    )(share, gain, *att, *msg, *mixes, *ups, *downs)


def gather_pieces(piece, axis):
    count = lax.axis_size(axis)
    pieces = {0: piece}
    bit = count // 2
    while bit:
        for k in list(pieces):
            pieces[k | bit] = lax.ppermute(pieces[k], axis, xor_route(count, bit))
        bit //= 2
    return [pieces[k] for k in range(count)]


def layer(
    x,
    mixer_gain,
    perceptron_gain,
    projectors,
    scale,
    out_projector,
    neighbour_projector,
    expand,
    contract,
    companion,
    sender,
    tally,
    landing,
    tail,
    sink,
):
    peers = lax.axis_size("dom")
    shares = lax.axis_size("mp")

    def send(block, mask):
        return lax.ppermute(block, "dom", xor_route(peers, mask))

    near = 1 << ((peers.bit_length() - 1) // 2)
    far = peers // near
    (
        low_mask, high_mask, pair, q, kv, k, v, mix, scales, quarter, share, late_gain, landing,
        *outgoing,
    ) = prologue(
        tally, companion, scale, x, mixer_gain[None, :], projectors, sender[0],
        out_projector, neighbour_projector, perceptron_gain[None, :], landing[0], near, shares,
    )
    ups = gather_pieces(expand, "mp")
    downs = gather_pieces(contract, "mp")
    mixes = gather_pieces(mix, "mp")
    nodes, edges = x.shape[0], tail.shape[1]

    def shared(outgoing, tail, sink):
        held = [outgoing[0]] + [send(outgoing[a], a) for a in range(1, near)]
        arrived = [send(block, h * near) for h, block in enumerate(pack(held), start=1)]
        counts = edge_counts(tail, sink, nodes, 0, edges)
        return counts, held[1:] + arrived

    origins = tuple((a - 1, 0, a) for a in range(1, near)) + tuple(
        (near - 2 + h, a, h * near + a) for h in range(1, far) for a in range(near)
    )
    operands = (kv, k, v, outgoing, tail, sink)
    if peers * (peers - 1) // 2 <= 32:
        branches = []
        for high in range(1, peers):
            for low in range(1, high):

                def branch(kv, k, v, *rest, low=low, high=high):
                    landed = shared(*rest)
                    if low & high & (peers // 2):
                        one_k, one_v = send(k, low), send(v, low)
                        two_k, two_v = send(one_k, low ^ high), send(one_v, low ^ high)
                        one = jnp.concatenate([one_k, one_v], axis=1)
                        two = jnp.concatenate([two_k, two_v], axis=1)
                    else:
                        one, two = send(kv, low), send(kv, high)
                    return (one, two) + landed

                branches.append(branch)
        one, two, counts, arrived = lax.switch(pair[0], branches, *operands)
    else:
        hops = [lambda kv, mask=mask: send(kv, mask) for mask in range(1, peers)]
        one = lax.switch(low_mask[0], hops, kv)
        two = lax.switch(high_mask[0], hops, kv)
        counts, arrived = shared(outgoing, tail, sink)

    msg = messages(counts, quarter, landing, arrived, origins, shares)

    def swap(chunk, k):
        return lax.ppermute(chunk, "mp", xor_route(shares, k)) if k else chunk

    msg = [swap(chunk, k) for k, chunk in enumerate(msg)]
    groups = [tuple(range(shares // 2, shares)), tuple(range(shares // 2))]
    att = [None] * shares
    for group in groups:
        chunks = attention(scales, q, kv, one, two, shares, group)
        for k, chunk in zip(group, chunks):
            att[k] = swap(chunk, k)
    return final(share, late_gain, att, msg, mixes, ups, downs)


def solution(mesh):
    return jax.shard_map(
        layer,
        mesh=mesh,
        in_specs=(
            P("dom", None),
            P(),
            P(),
            P(None, None, "mp"),
            P("mp"),
            P("mp", None),
            P("mp", None),
            P(None, "mp"),
            P("mp", None),
            P(),
            P("dom", None, None),
            P("dom", None),
            P("dom", None, None),
            P("dom", None),
            P("dom", None),
        ),
        out_specs=P(("dom", "mp"), None),
        check_vma=False,
    )
```

```python
import functools
import math

import jax
import jax.numpy as jnp
from jax import lax
from jax.experimental import pallas as pl
from jax.experimental.pallas import tpu as pltpu
from jax.sharding import PartitionSpec as P


HEAD_SIZE = 64
EPSILON = 1e-05
FLAG_ROWS = 8
EDGE_STEP = 512

f32 = jnp.float32
bf16 = jnp.bfloat16
f8 = jnp.float8_e4m3fn

VMEM = pl.BlockSpec(memory_space=pltpu.VMEM)
SMEM = pl.BlockSpec(memory_space=pltpu.SMEM)
HBM = pl.BlockSpec(memory_space=pltpu.HBM)

NT = (((1,), (1,)), ((), ()))
NN = (((1,), (0,)), ((), ()))

PARAMS = pltpu.CompilerParams(vmem_limit_bytes=24 << 20)


def dot(a, b, dims=NN):
    return lax.dot_general(a, b, dims, preferred_element_type=f32)


def norm_rows(rows, gain):
    mean = jnp.mean(rows, -1, keepdims=True)
    centred = rows - mean
    variance = jnp.mean(centred * centred, -1, keepdims=True)
    return (centred * lax.rsqrt(variance + EPSILON) * gain).astype(bf16)


def one_hot_columns(index_row, count, live=None):
    hit = lax.broadcasted_iota(jnp.int32, (count, index_row.shape[1]), 0) == index_row
    if live is not None:
        hit = jnp.logical_and(hit, live)
    return jnp.where(hit, 1.0, 0.0).astype(bf16)


def narrow_one_hot(index_row, count):
    numbers = lax.broadcasted_iota(jnp.int16, (count, index_row.shape[1]), 0)
    hit = numbers == index_row.astype(jnp.int16)
    return jnp.where(hit, jnp.ones((), bf16), jnp.zeros((), bf16)).astype(f8)


def in_hbm(*arrays):
    return [pltpu.with_memory_space_constraint(array, pltpu.HBM) for array in arrays]


def xor_route(count, mask):
    return [(i, i ^ mask) for i in range(count)]


def prologue_kernel(
    x_hbm, gain_hbm, w_hbm, sender_hbm, up_hbm, down_hbm, wo_hbm, wn_hbm, late_gain_hbm, landing_hbm,
    tally_hbm, companion_hbm, scale_hbm,
    low_ref, high_ref, pair_ref, q_ref, kv_ref, k_ref, v_ref, bundle_ref, scales_ref,
    share_ref, late_gain_ref, landing_ref, *rest,
):
    out_refs = rest[:-8]
    x_ref, gain_ref, w_ref, sender_ref, tally_ref, companion_ref, scale_ref, sems = rest[-8:]
    nodes, _ = x_ref.shape
    cols = q_ref.shape[1]
    sources = (
        (x_hbm, x_ref),
        (gain_hbm, gain_ref),
        (w_hbm, w_ref),
        (sender_hbm, sender_ref),
        (late_gain_hbm, late_gain_ref),
        (landing_hbm, landing_ref),
        (tally_hbm, tally_ref),
        (companion_hbm, companion_ref),
        (scale_hbm, scale_ref),
    )
    first = 0
    for piece in (up_hbm, down_hbm, wo_hbm, wn_hbm):
        sources += ((piece, bundle_ref.at[pl.ds(first, piece.shape[0])]),)
        first += piece.shape[0]
    copies = [
        pltpu.make_async_copy(source, target, sems.at[i])
        for i, (source, target) in enumerate(sources)
    ]
    for copy in copies:
        copy.start()

    copies[0].wait()
    copies[1].wait()
    normed = norm_rows(x_ref[...].astype(f32), gain_ref[...])
    copies[2].wait()
    weights = jnp.concatenate([w_ref[0], w_ref[1], w_ref[2]], axis=1)
    projected = dot(normed, weights).astype(bf16)
    q_ref[...] = projected[:, :cols]
    kv_ref[...] = projected[:, cols:]
    k_ref[...] = projected[:, cols : 2 * cols]
    v_ref[...] = projected[:, 2 * cols :]

    for copy in copies[3:-4]:
        copy.wait()
    one, two = companion_ref[0, 0], companion_ref[1, 0]
    low, high = jnp.minimum(one, two), jnp.maximum(one, two)
    low_ref[0] = low - 1
    high_ref[0] = high - 1
    pair_ref[0] = lax.shift_right_logical((high - 1) * (high - 2), 1) + low - 1
    for h in range(scales_ref.shape[0]):
        scales_ref[h] = jnp.full(scales_ref.shape[1:], scale_ref[h], f32)

    part = lax.axis_index("mp")
    rows = share_ref.shape[0]
    share_ref[...] = x_ref[pl.ds(pl.multiple_of(part * rows, rows), rows), :]
    quarter = x_ref[:, pl.ds(pl.multiple_of(part * cols, 128), cols)]
    quarter_t = quarter.astype(f32).T.astype(bf16)
    cap = sender_ref.shape[1]
    slot = lax.broadcasted_iota(jnp.int32, (1, cap), 1)
    (out_ref,) = out_refs
    for dest in range(out_ref.shape[0]):
        live = slot < tally_ref[0, dest]
        pick = one_hot_columns(sender_ref[dest : dest + 1, :], nodes, live)
        out_ref[dest, :cols, :] = dot(quarter_t, pick).astype(bf16)
        out_ref[dest, cols:, :] = jnp.broadcast_to(
            jnp.where(live, 1.0, 0.0), (FLAG_ROWS, cap)
        ).astype(bf16)
    for copy in copies[-4:]:
        copy.wait()


def prologue(
    tally, companion, scale, x, gain, w, sender, pieces, late_gain, landing, shares
):
    nodes, width = x.shape
    cols = w.shape[2]
    peers, cap = sender.shape
    return pl.pallas_call(
        prologue_kernel,
        out_shape=[jax.ShapeDtypeStruct((1,), jnp.int32)] * 3
        + [jax.ShapeDtypeStruct((nodes, n * cols), bf16) for n in (1, 2, 1, 1)]
        + [
            jax.ShapeDtypeStruct((sum(p.shape[0] for p in pieces), width), bf16),
            jax.ShapeDtypeStruct((scale.shape[0], 8, 128), f32),
            jax.ShapeDtypeStruct((nodes // shares, width), bf16),
            jax.ShapeDtypeStruct(late_gain.shape, f32),
            jax.ShapeDtypeStruct(landing.shape, jnp.int32),
        ]
        + [jax.ShapeDtypeStruct((peers, cols + FLAG_ROWS, cap), bf16)],
        in_specs=[HBM] * (9 + len(pieces)),
        out_specs=[SMEM] * 3 + [VMEM] * 10,
        scratch_shapes=[
            pltpu.VMEM(x.shape, bf16),
            pltpu.VMEM(gain.shape, f32),
            pltpu.VMEM(w.shape, bf16),
            pltpu.VMEM(sender.shape, jnp.int32),
            pltpu.SMEM(tally.shape, jnp.int32),
            pltpu.SMEM(companion.shape, jnp.int32),
            pltpu.SMEM(scale.shape, f32),
            pltpu.SemaphoreType.DMA((9 + len(pieces),)),
        ],
        name="prologue",
        compiler_params=PARAMS,
        cost_estimate=pl.CostEstimate(
            flops=2 * nodes * width * 3 * cols, bytes_accessed=4 << 20, transcendentals=0
        ),
    )(
        *in_hbm(
            x, gain, w, sender, *pieces, late_gain, landing, tally, companion, scale
        )
    )


def edge_kernel(
    tail_hbm, sink_hbm, x_hbm, local_ref, degree_ref, tail_ref, sink_ref, x_ref, counts_ref, sems
):
    copies = [
        pltpu.make_async_copy(tail_hbm, tail_ref, sems.at[0]),
        pltpu.make_async_copy(sink_hbm, sink_ref, sems.at[1]),
        pltpu.make_async_copy(x_hbm, x_ref, sems.at[2]),
    ]
    for copy in copies:
        copy.start()
    nodes, rows = counts_ref.shape
    edges = tail_ref.shape[1]
    step = math.gcd(edges, EDGE_STEP)
    first = lax.axis_index("mp") * rows
    counts_ref[...] = jnp.zeros_like(counts_ref)
    copies[0].wait()
    copies[1].wait()

    def add(turn, unused):
        at = pl.ds(pl.multiple_of(turn * step, step), step)
        tail = narrow_one_hot(tail_ref[:, at], nodes)
        sink = narrow_one_hot(sink_ref[:, at] - first, rows)
        counts_ref[...] += dot(tail, sink, NT)
        return unused

    lax.fori_loop(0, edges // step, add, 0)
    counts = counts_ref[...].T
    high = jnp.floor(counts * (1.0 / 256.0))
    low = counts - 256.0 * high
    pair = jnp.concatenate([high, low], axis=0).astype(bf16)
    copies[2].wait()
    sums = dot(pair, x_ref[...])
    own = x_ref[pl.ds(pl.multiple_of(first, rows), rows), :]
    local_ref[...] = 256.0 * sums[:rows] + sums[rows:] + own.astype(f32)
    degree = jnp.sum(counts, -1, keepdims=True)
    degree_ref[...] = jnp.broadcast_to(1.0 + degree, degree_ref.shape)


def edge_sums(tail, sink, x, rows):
    edges = tail.shape[1]
    nodes, width = x.shape
    return pl.pallas_call(
        edge_kernel,
        out_shape=[
            jax.ShapeDtypeStruct((rows, width), f32),
            jax.ShapeDtypeStruct((rows, 128), f32),
        ],
        in_specs=[HBM] * 3,
        out_specs=[VMEM] * 2,
        scratch_shapes=[
            pltpu.VMEM((1, edges), jnp.int32),
            pltpu.VMEM((1, edges), jnp.int32),
            pltpu.VMEM((nodes, width), bf16),
            pltpu.VMEM((nodes, rows), f32),
            pltpu.SemaphoreType.DMA((3,)),
        ],
        name="edge_sums",
        compiler_params=PARAMS,
        cost_estimate=pl.CostEstimate(
            flops=2 * nodes * nodes * edges, bytes_accessed=2 << 20, transcendentals=0
        ),
    )(*in_hbm(tail, sink, x))


def landing_kernel(edge_degree_ref, landing_ref, arrived_ref, degree_ref, *refs):
    outs, whole_ref = refs[:-1], refs[-1]
    part = lax.axis_index("mp")
    nodes = whole_ref.shape[0]
    rows, cols = outs[0].shape
    peers = arrived_ref.shape[0]
    land = jnp.concatenate(
        [one_hot_columns(landing_ref[p : p + 1, :], nodes) for p in range(peers)], axis=1
    )
    arrived = jnp.concatenate([arrived_ref[p] for p in range(peers)], axis=1)
    boundary = dot(land, arrived, NT)
    whole_ref[:, : boundary.shape[1]] = boundary
    for k, out_ref in enumerate(outs):
        at = jnp.bitwise_xor(part, k) * rows
        out_ref[...] = whole_ref[pl.ds(pl.multiple_of(at, rows), rows), :cols]
    own = pl.ds(pl.multiple_of(part * rows, rows), rows)
    degree_ref[...] = edge_degree_ref[...] + whole_ref[own, cols : cols + 1]


def landed_sums(edge_degree, landing, arrived, nodes, cols, shares):
    rows = nodes // shares
    return pl.pallas_call(
        landing_kernel,
        out_shape=[jax.ShapeDtypeStruct((rows, 128), f32)]
        + [jax.ShapeDtypeStruct((rows, cols), f32)] * shares,
        in_specs=[VMEM] * 3,
        out_specs=[VMEM] * (1 + shares),
        scratch_shapes=[pltpu.VMEM((nodes, 2 * cols), f32)],
        name="landing",
        compiler_params=PARAMS,
        cost_estimate=pl.CostEstimate(
            flops=2 * nodes * 1024 * 256, bytes_accessed=2 << 20, transcendentals=0
        ),
    )(edge_degree, landing, arrived)


def attention_kernel(
    offsets, scales_ref, q_ref, own_ref, one_any, two_any, *refs
):
    outs, (one_ref, two_ref, block_ref, sems) = refs[:-4], refs[-4:]
    copies = [
        pltpu.make_async_copy(one_any, one_ref, sems.at[0]),
        pltpu.make_async_copy(two_any, two_ref, sems.at[1]),
    ]
    for copy in copies:
        copy.start()
    part = lax.axis_index("mp")
    rows, cols = outs[0].shape
    heads = cols // HEAD_SIZE
    count = len(offsets)
    base = jnp.bitwise_xor(part, offsets[0]) // count * count
    at = pl.multiple_of(base * rows, count * rows)
    sources = (own_ref, one_ref, two_ref)
    for h in range(heads):
        band = slice(h * HEAD_SIZE, (h + 1) * HEAD_SIZE)
        q = q_ref[pl.ds(at, count * rows), band]
        factor = scales_ref[h, :1, :1] * math.log2(math.e)
        parts = []
        for i, r in enumerate(sources):
            if h == 0 and i > 0:
                copies[i - 1].wait()
            parts.append(dot(q, r[:, band], NT) * factor)
        top = functools.reduce(jnp.maximum, [jnp.max(s, -1, keepdims=True) for s in parts])
        powers = [jnp.exp2(s - top) for s in parts]
        inverse = 1.0 / sum(jnp.sum(p, -1, keepdims=True) for p in powers)
        value_band = slice(cols + h * HEAD_SIZE, cols + (h + 1) * HEAD_SIZE)
        attended = sum(
            dot((p * inverse).astype(bf16), r[:, value_band]) for p, r in zip(powers, sources)
        )
        block_ref[:, band] = attended.astype(bf16)
    for k, out_ref in zip(offsets, outs):
        place = (jnp.bitwise_xor(part, k) - base) * rows
        out_ref[...] = block_ref[pl.ds(pl.multiple_of(place, rows), rows), :]


def attention(scales, q, own, one, two, shares, offsets):
    nodes, cols = q.shape
    rows = nodes // shares
    any_space = pl.BlockSpec(memory_space=pl.ANY)
    return pl.pallas_call(
        functools.partial(attention_kernel, offsets),
        out_shape=[jax.ShapeDtypeStruct((rows, cols), bf16)] * len(offsets),
        in_specs=[VMEM] * 3 + [any_space] * 2,
        out_specs=[VMEM] * len(offsets),
        scratch_shapes=[
            pltpu.VMEM(one.shape, bf16),
            pltpu.VMEM(two.shape, bf16),
            pltpu.VMEM((len(offsets) * rows, cols), bf16),
            pltpu.SemaphoreType.DMA((2,)),
        ],
        name="attention",
        compiler_params=PARAMS,
        cost_estimate=pl.CostEstimate(
            flops=4 * rows * len(offsets) * 3 * nodes * 256,
            bytes_accessed=2 << 20,
            transcendentals=1 << 20,
        ),
    )(scales, q, own, one, two)


def final_kernel(shares, share_ref, gain_ref, local_ref, degree_ref, *refs):
    att, far_sums, bundles = (refs[i * shares : (i + 1) * shares] for i in range(3))
    out_ref, mix_buf, up_buf, down_buf, sems = refs[3 * shares :]
    _, width = out_ref.shape
    wide = up_buf.shape[2]
    mix_at, up_at, down_at = (
        pl.ds(width + wide, mix_buf.shape[1]), pl.ds(0, width), pl.ds(width, wide)
    )
    copies = []
    for i, (at, buf) in enumerate(((mix_at, mix_buf), (up_at, up_buf), (down_at, down_buf))):
        copies.append(
            [
                pltpu.make_async_copy(source.at[at], buf.at[k], sems.at[i, k])
                for k, source in enumerate(bundles)
            ]
        )
    for copy in copies[0]:
        copy.start()
    for k in range(shares):
        copies[1][k].start()
        copies[2][k].start()
    mixed = share_ref[...].astype(f32)
    part = lax.axis_index("mp")
    cols = att[0].shape[1]
    terms = []
    for k in range(shares):
        at = pl.multiple_of(jnp.bitwise_xor(part, k) * cols, 128)
        sums = local_ref[:, pl.ds(at, cols)] + far_sums[k][...]
        terms += [att[k][...], (sums / degree_ref[...]).astype(bf16)]
    terms = jnp.concatenate(terms, axis=1)
    for copy in copies[0]:
        copy.wait()
    mixed = mixed + dot(terms, mix_buf[...].reshape(-1, width))
    normed = norm_rows(mixed, gain_ref[...])
    total = mixed
    for k in range(shares):
        copies[1][k].wait()
        wide = dot(normed, up_buf[k])
        hidden = (0.5 * wide * (1.0 + lax.erf(wide * (0.5**0.5)))).astype(bf16)
        copies[2][k].wait()
        total = total + dot(hidden, down_buf[k])
    out_ref[...] = total.astype(bf16)


def final(share, gain, local, degree, att, far_sums, bundles):
    shares = len(att)
    rows, width = share.shape
    cols = att[0].shape[1]
    wide = bundles[0].shape[0] - width - 2 * cols
    any_space = pl.BlockSpec(memory_space=pl.ANY)
    return pl.pallas_call(
        functools.partial(final_kernel, shares),
        out_shape=jax.ShapeDtypeStruct((rows, width), bf16),
        in_specs=[VMEM] * (4 + 2 * shares) + [any_space] * shares,
        out_specs=VMEM,
        scratch_shapes=[
            pltpu.VMEM((shares, *shape), bf16)
            for shape in ((2 * cols, width), (width, wide), (wide, width))
        ]
        + [pltpu.SemaphoreType.DMA((3, shares))],
        name="final",
        compiler_params=PARAMS,
        cost_estimate=pl.CostEstimate(
            flops=2 * rows * width * 4096, bytes_accessed=6 << 20, transcendentals=1 << 18
        ),
    )(share, gain, local, degree, *att, *far_sums, *bundles)


def gather_pieces(piece, axis):
    count = lax.axis_size(axis)
    pieces = {0: piece}
    bit = count // 2
    while bit:
        for k in list(pieces):
            pieces[k | bit] = lax.ppermute(pieces[k], axis, xor_route(count, bit))
        bit //= 2
    return [pieces[k] for k in range(count)]


def layer(
    x,
    mixer_gain,
    perceptron_gain,
    projectors,
    scale,
    out_projector,
    neighbour_projector,
    expand,
    contract,
    companion,
    sender,
    tally,
    landing,
    tail,
    sink,
):
    peers = lax.axis_size("dom")
    shares = lax.axis_size("mp")
    cols = projectors.shape[2]

    def send(block, mask):
        return lax.ppermute(block, "dom", xor_route(peers, mask))

    (
        low_mask, high_mask, pair, q, kv, k, v, bundle, scales, share, late_gain, landing,
        outgoing,
    ) = prologue(
        tally, companion, scale, x, mixer_gain[None, :], projectors, sender[0],
        (expand, contract, out_projector, neighbour_projector), perceptron_gain[None, :],
        landing[0], shares,
    )
    bundles = gather_pieces(bundle, "mp")
    nodes = x.shape[0]

    def beside(outgoing, tail, sink, x):
        arrived = lax.all_to_all(outgoing, "dom", split_axis=0, concat_axis=0, tiled=True)
        return arrived, *edge_sums(tail, sink, x, nodes // shares)

    operands = (kv, k, v, outgoing, tail, sink, x)
    if peers * (peers - 1) // 2 <= 32:
        branches = []
        for high in range(1, peers):
            for low in range(1, high):

                def branch(kv, k, v, *rest, low=low, high=high):
                    if low & high & (peers // 2):
                        one_k, one_v = send(k, low), send(v, low)
                        two_k, two_v = send(one_k, low ^ high), send(one_v, low ^ high)
                        one = jnp.concatenate([one_k, one_v], axis=1)
                        two = jnp.concatenate([two_k, two_v], axis=1)
                    else:
                        one, two = send(kv, low), send(kv, high)
                    return one, two, *beside(*rest)

                branches.append(branch)
        one, two, arrived, local, edge_degree = lax.switch(pair[0], branches, *operands)
    else:
        hops = [lambda kv, mask=mask: send(kv, mask) for mask in range(1, peers)]
        one = lax.switch(low_mask[0], hops, kv)
        two = lax.switch(high_mask[0], hops, kv)
        arrived, local, edge_degree = beside(outgoing, tail, sink, x)

    degree, *far_sums = landed_sums(edge_degree, landing, arrived, nodes, cols, shares)

    def swap(chunk, k):
        return lax.ppermute(chunk, "mp", xor_route(shares, k)) if k else chunk

    far_sums = [swap(chunk, k) for k, chunk in enumerate(far_sums)]
    groups = [tuple(range(shares // 2, shares)), tuple(range(shares // 2))]
    att = [None] * shares
    for group in groups:
        chunks = attention(scales, q, kv, one, two, shares, group)
        for k, chunk in zip(group, chunks):
            att[k] = swap(chunk, k)
    return final(share, late_gain, local, degree, att, far_sums, bundles)


def solution(mesh):
    return jax.shard_map(
        layer,
        mesh=mesh,
        in_specs=(
            P("dom", None),
            P(),
            P(),
            P(None, None, "mp"),
            P("mp"),
            P("mp", None),
            P("mp", None),
            P(None, "mp"),
            P("mp", None),
            P(),
            P("dom", None, None),
            P("dom", None),
            P("dom", None, None),
            P("dom", None),
            P("dom", None),
        ),
        out_specs=P(("dom", "mp"), None),
        check_vma=False,
    )
```

```python
import functools
import math

import jax
import jax.numpy as jnp
from jax import lax
from jax.experimental import pallas as pl
from jax.experimental.pallas import tpu as pltpu
from jax.sharding import PartitionSpec as P


HEAD_SIZE = 64
EPSILON = 1e-05
FLAG_ROWS = 8
EDGE_STEP = 512
EDGE_STEP_ON_PATH = 1024

f32 = jnp.float32
bf16 = jnp.bfloat16
f8 = jnp.float8_e4m3fn

VMEM = pl.BlockSpec(memory_space=pltpu.VMEM)
SMEM = pl.BlockSpec(memory_space=pltpu.SMEM)
HBM = pl.BlockSpec(memory_space=pltpu.HBM)

NT = (((1,), (1,)), ((), ()))
NN = (((1,), (0,)), ((), ()))

PARAMS = pltpu.CompilerParams(vmem_limit_bytes=24 << 20)


def dot(a, b, dims=NN):
    return lax.dot_general(a, b, dims, preferred_element_type=f32)


def norm_rows(rows, gain):
    mean = jnp.mean(rows, -1, keepdims=True)
    centred = rows - mean
    variance = jnp.mean(centred * centred, -1, keepdims=True)
    return (centred * lax.rsqrt(variance + EPSILON) * gain).astype(bf16)


def one_hot_columns(index_row, count, live=None):
    hit = lax.broadcasted_iota(jnp.int32, (count, index_row.shape[1]), 0) == index_row
    if live is not None:
        hit = jnp.logical_and(hit, live)
    return jnp.where(hit, 1.0, 0.0).astype(bf16)


def narrow_one_hot(index_row, count):
    numbers = lax.broadcasted_iota(jnp.int16, (count, index_row.shape[1]), 0)
    hit = numbers == index_row.astype(jnp.int16)
    return jnp.where(hit, jnp.ones((), bf16), jnp.zeros((), bf16)).astype(f8)


def in_hbm(*arrays):
    return [pltpu.with_memory_space_constraint(array, pltpu.HBM) for array in arrays]


def xor_route(count, mask):
    return [(i, i ^ mask) for i in range(count)]


def prologue_kernel(
    x_hbm, gain_hbm, w_hbm, sender_hbm, up_hbm, down_hbm, wo_hbm, wn_hbm, late_gain_hbm, landing_hbm,
    tally_hbm, companion_hbm, scale_hbm,
    low_ref, high_ref, pair_ref, q_ref, kv_ref, k_ref, v_ref, bundle_ref, scales_ref,
    share_ref, late_gain_ref, landing_ref, *rest,
):
    out_refs = rest[:-8]
    x_ref, gain_ref, w_ref, sender_ref, tally_ref, companion_ref, scale_ref, sems = rest[-8:]
    nodes, _ = x_ref.shape
    cols = q_ref.shape[1]
    sources = (
        (x_hbm, x_ref),
        (gain_hbm, gain_ref),
        (w_hbm, w_ref),
        (sender_hbm, sender_ref),
        (late_gain_hbm, late_gain_ref),
        (landing_hbm, landing_ref),
        (tally_hbm, tally_ref),
        (companion_hbm, companion_ref),
        (scale_hbm, scale_ref),
    )
    first = 0
    for piece in (up_hbm, down_hbm, wo_hbm, wn_hbm):
        sources += ((piece, bundle_ref.at[pl.ds(first, piece.shape[0])]),)
        first += piece.shape[0]
    copies = [
        pltpu.make_async_copy(source, target, sems.at[i])
        for i, (source, target) in enumerate(sources)
    ]
    for copy in copies:
        copy.start()

    copies[0].wait()
    copies[1].wait()
    normed = norm_rows(x_ref[...].astype(f32), gain_ref[...])
    copies[2].wait()
    weights = jnp.concatenate([w_ref[0], w_ref[1], w_ref[2]], axis=1)
    projected = dot(normed, weights).astype(bf16)
    q_ref[...] = projected[:, :cols]
    kv_ref[...] = projected[:, cols:]
    k_ref[...] = projected[:, cols : 2 * cols]
    v_ref[...] = projected[:, 2 * cols :]

    for copy in copies[3:-4]:
        copy.wait()
    one, two = companion_ref[0, 0], companion_ref[1, 0]
    low, high = jnp.minimum(one, two), jnp.maximum(one, two)
    low_ref[0] = low - 1
    high_ref[0] = high - 1
    pair_ref[0] = lax.shift_right_logical((high - 1) * (high - 2), 1) + low - 1
    for h in range(scales_ref.shape[0]):
        scales_ref[h] = jnp.full(scales_ref.shape[1:], scale_ref[h], f32)

    part = lax.axis_index("mp")
    rows = share_ref.shape[0]
    share_ref[...] = x_ref[pl.ds(pl.multiple_of(part * rows, rows), rows), :]
    quarter = x_ref[:, pl.ds(pl.multiple_of(part * cols, 128), cols)]
    quarter_t = quarter.astype(f32).T.astype(bf16)
    cap = sender_ref.shape[1]
    slot = lax.broadcasted_iota(jnp.int32, (1, cap), 1)
    (out_ref,) = out_refs
    for dest in range(out_ref.shape[0]):
        live = slot < tally_ref[0, dest]
        pick = one_hot_columns(sender_ref[dest : dest + 1, :], nodes, live)
        out_ref[dest, :cols, :] = dot(quarter_t, pick).astype(bf16)
        out_ref[dest, cols:, :] = jnp.broadcast_to(
            jnp.where(live, 1.0, 0.0), (FLAG_ROWS, cap)
        ).astype(bf16)
    for copy in copies[-4:]:
        copy.wait()


def prologue(
    tally, companion, scale, x, gain, w, sender, pieces, late_gain, landing, shares
):
    nodes, width = x.shape
    cols = w.shape[2]
    peers, cap = sender.shape
    return pl.pallas_call(
        prologue_kernel,
        out_shape=[jax.ShapeDtypeStruct((1,), jnp.int32)] * 3
        + [jax.ShapeDtypeStruct((nodes, n * cols), bf16) for n in (1, 2, 1, 1)]
        + [
            jax.ShapeDtypeStruct((sum(p.shape[0] for p in pieces), width), bf16),
            jax.ShapeDtypeStruct((scale.shape[0], 8, 128), f32),
            jax.ShapeDtypeStruct((nodes // shares, width), bf16),
            jax.ShapeDtypeStruct(late_gain.shape, f32),
            jax.ShapeDtypeStruct(landing.shape, jnp.int32),
        ]
        + [jax.ShapeDtypeStruct((peers, cols + FLAG_ROWS, cap), bf16)],
        in_specs=[HBM] * (9 + len(pieces)),
        out_specs=[SMEM] * 3 + [VMEM] * 10,
        scratch_shapes=[
            pltpu.VMEM(x.shape, bf16),
            pltpu.VMEM(gain.shape, f32),
            pltpu.VMEM(w.shape, bf16),
            pltpu.VMEM(sender.shape, jnp.int32),
            pltpu.SMEM(tally.shape, jnp.int32),
            pltpu.SMEM(companion.shape, jnp.int32),
            pltpu.SMEM(scale.shape, f32),
            pltpu.SemaphoreType.DMA((9 + len(pieces),)),
        ],
        name="prologue",
        compiler_params=PARAMS,
        cost_estimate=pl.CostEstimate(
            flops=2 * nodes * width * 3 * cols, bytes_accessed=4 << 20, transcendentals=0
        ),
    )(
        *in_hbm(
            x, gain, w, sender, *pieces, late_gain, landing, tally, companion, scale
        )
    )


def edge_kernel(
    most, tail_hbm, sink_hbm, x_hbm, local_ref, degree_ref, tail_ref, sink_ref, x_ref, counts_ref, sems
):
    copies = [
        pltpu.make_async_copy(tail_hbm, tail_ref, sems.at[0]),
        pltpu.make_async_copy(sink_hbm, sink_ref, sems.at[1]),
        pltpu.make_async_copy(x_hbm, x_ref, sems.at[2]),
    ]
    for copy in copies:
        copy.start()
    nodes, rows = counts_ref.shape
    edges = tail_ref.shape[1]
    step = math.gcd(edges, most)
    first = lax.axis_index("mp") * rows
    counts_ref[...] = jnp.zeros_like(counts_ref)
    copies[0].wait()
    copies[1].wait()

    def add(turn, unused):
        at = pl.ds(pl.multiple_of(turn * step, step), step)
        tail = narrow_one_hot(tail_ref[:, at], nodes)
        sink = narrow_one_hot(sink_ref[:, at] - first, rows)
        counts_ref[...] += dot(tail, sink, NT)
        return unused

    lax.fori_loop(0, edges // step, add, 0)
    counts = counts_ref[...].T
    high = jnp.floor(counts * (1.0 / 256.0))
    low = counts - 256.0 * high
    pair = jnp.concatenate([high, low], axis=0).astype(bf16)
    copies[2].wait()
    sums = dot(pair, x_ref[...])
    own = x_ref[pl.ds(pl.multiple_of(first, rows), rows), :]
    local_ref[...] = 256.0 * sums[:rows] + sums[rows:] + own.astype(f32)
    degree = jnp.sum(counts, -1, keepdims=True)
    degree_ref[...] = jnp.broadcast_to(1.0 + degree, degree_ref.shape)


def edge_sums(tail, sink, x, rows, most):
    edges = tail.shape[1]
    nodes, width = x.shape
    return pl.pallas_call(
        functools.partial(edge_kernel, most),
        out_shape=[
            jax.ShapeDtypeStruct((rows, width), f32),
            jax.ShapeDtypeStruct((rows, 128), f32),
        ],
        in_specs=[HBM] * 3,
        out_specs=[VMEM] * 2,
        scratch_shapes=[
            pltpu.VMEM((1, edges), jnp.int32),
            pltpu.VMEM((1, edges), jnp.int32),
            pltpu.VMEM((nodes, width), bf16),
            pltpu.VMEM((nodes, rows), f32),
            pltpu.SemaphoreType.DMA((3,)),
        ],
        name="edge_sums",
        compiler_params=PARAMS,
        cost_estimate=pl.CostEstimate(
            flops=2 * nodes * nodes * edges, bytes_accessed=2 << 20, transcendentals=0
        ),
    )(*in_hbm(tail, sink, x))


def landing_kernel(edge_degree_ref, landing_ref, arrived_ref, degree_ref, *refs):
    outs, whole_ref = refs[:-1], refs[-1]
    part = lax.axis_index("mp")
    nodes = whole_ref.shape[0]
    rows, cols = outs[0].shape
    peers = arrived_ref.shape[0]
    land = jnp.concatenate(
        [one_hot_columns(landing_ref[p : p + 1, :], nodes) for p in range(peers)], axis=1
    )
    arrived = jnp.concatenate([arrived_ref[p] for p in range(peers)], axis=1)
    boundary = dot(land, arrived, NT)
    whole_ref[:, : boundary.shape[1]] = boundary
    for k, out_ref in enumerate(outs):
        at = jnp.bitwise_xor(part, k) * rows
        out_ref[...] = whole_ref[pl.ds(pl.multiple_of(at, rows), rows), :cols]
    own = pl.ds(pl.multiple_of(part * rows, rows), rows)
    degree_ref[...] = edge_degree_ref[...] + whole_ref[own, cols : cols + 1]


def landed_sums(edge_degree, landing, arrived, nodes, cols, shares):
    rows = nodes // shares
    return pl.pallas_call(
        landing_kernel,
        out_shape=[jax.ShapeDtypeStruct((rows, 128), f32)]
        + [jax.ShapeDtypeStruct((rows, cols), f32)] * shares,
        in_specs=[VMEM] * 3,
        out_specs=[VMEM] * (1 + shares),
        scratch_shapes=[pltpu.VMEM((nodes, 2 * cols), f32)],
        name="landing",
        compiler_params=PARAMS,
        cost_estimate=pl.CostEstimate(
            flops=2 * nodes * 1024 * 256, bytes_accessed=2 << 20, transcendentals=0
        ),
    )(edge_degree, landing, arrived)


def attention_kernel(
    offsets, scales_ref, q_ref, own_ref, one_any, two_any, *refs
):
    outs, (one_ref, two_ref, block_ref, sems) = refs[:-4], refs[-4:]
    copies = [
        pltpu.make_async_copy(one_any, one_ref, sems.at[0]),
        pltpu.make_async_copy(two_any, two_ref, sems.at[1]),
    ]
    for copy in copies:
        copy.start()
    part = lax.axis_index("mp")
    rows, cols = outs[0].shape
    heads = cols // HEAD_SIZE
    count = len(offsets)
    base = jnp.bitwise_xor(part, offsets[0]) // count * count
    at = pl.multiple_of(base * rows, count * rows)
    sources = (own_ref, one_ref, two_ref)
    for h in range(heads):
        band = slice(h * HEAD_SIZE, (h + 1) * HEAD_SIZE)
        q = q_ref[pl.ds(at, count * rows), band]
        factor = scales_ref[h, :1, :1] * math.log2(math.e)
        parts = []
        for i, r in enumerate(sources):
            if h == 0 and i > 0:
                copies[i - 1].wait()
            parts.append(dot(q, r[:, band], NT) * factor)
        top = functools.reduce(jnp.maximum, [jnp.max(s, -1, keepdims=True) for s in parts])
        powers = [jnp.exp2(s - top) for s in parts]
        inverse = 1.0 / sum(jnp.sum(p, -1, keepdims=True) for p in powers)
        value_band = slice(cols + h * HEAD_SIZE, cols + (h + 1) * HEAD_SIZE)
        attended = sum(
            dot((p * inverse).astype(bf16), r[:, value_band]) for p, r in zip(powers, sources)
        )
        block_ref[:, band] = attended.astype(bf16)
    for k, out_ref in zip(offsets, outs):
        place = (jnp.bitwise_xor(part, k) - base) * rows
        out_ref[...] = block_ref[pl.ds(pl.multiple_of(place, rows), rows), :]


def attention(scales, q, own, one, two, shares, offsets):
    nodes, cols = q.shape
    rows = nodes // shares
    any_space = pl.BlockSpec(memory_space=pl.ANY)
    return pl.pallas_call(
        functools.partial(attention_kernel, offsets),
        out_shape=[jax.ShapeDtypeStruct((rows, cols), bf16)] * len(offsets),
        in_specs=[VMEM] * 3 + [any_space] * 2,
        out_specs=[VMEM] * len(offsets),
        scratch_shapes=[
            pltpu.VMEM(one.shape, bf16),
            pltpu.VMEM(two.shape, bf16),
            pltpu.VMEM((len(offsets) * rows, cols), bf16),
            pltpu.SemaphoreType.DMA((2,)),
        ],
        name="attention",
        compiler_params=PARAMS,
        cost_estimate=pl.CostEstimate(
            flops=4 * rows * len(offsets) * 3 * nodes * 256,
            bytes_accessed=2 << 20,
            transcendentals=1 << 20,
        ),
    )(scales, q, own, one, two)


def final_kernel(shares, share_ref, gain_ref, local_ref, degree_ref, *refs):
    att, far_sums, bundles = (refs[i * shares : (i + 1) * shares] for i in range(3))
    out_ref, mix_buf, up_buf, down_buf, sems = refs[3 * shares :]
    _, width = out_ref.shape
    wide = up_buf.shape[2]
    mix_at, up_at, down_at = (
        pl.ds(width + wide, mix_buf.shape[1]), pl.ds(0, width), pl.ds(width, wide)
    )
    copies = []
    for i, (at, buf) in enumerate(((mix_at, mix_buf), (up_at, up_buf), (down_at, down_buf))):
        copies.append(
            [
                pltpu.make_async_copy(source.at[at], buf.at[k], sems.at[i, k])
                for k, source in enumerate(bundles)
            ]
        )
    for copy in copies[0]:
        copy.start()
    for k in range(shares):
        copies[1][k].start()
        copies[2][k].start()
    mixed = share_ref[...].astype(f32)
    part = lax.axis_index("mp")
    cols = att[0].shape[1]
    terms = []
    for k in range(shares):
        at = pl.multiple_of(jnp.bitwise_xor(part, k) * cols, 128)
        sums = local_ref[:, pl.ds(at, cols)] + far_sums[k][...]
        terms += [att[k][...], (sums / degree_ref[...]).astype(bf16)]
    terms = jnp.concatenate(terms, axis=1)
    for copy in copies[0]:
        copy.wait()
    mixed = mixed + dot(terms, mix_buf[...].reshape(-1, width))
    normed = norm_rows(mixed, gain_ref[...])
    total = mixed
    for k in range(shares):
        copies[1][k].wait()
        wide = dot(normed, up_buf[k])
        hidden = (0.5 * wide * (1.0 + lax.erf(wide * (0.5**0.5)))).astype(bf16)
        copies[2][k].wait()
        total = total + dot(hidden, down_buf[k])
    out_ref[...] = total.astype(bf16)


def final(share, gain, local, degree, att, far_sums, bundles):
    shares = len(att)
    rows, width = share.shape
    cols = att[0].shape[1]
    wide = bundles[0].shape[0] - width - 2 * cols
    any_space = pl.BlockSpec(memory_space=pl.ANY)
    return pl.pallas_call(
        functools.partial(final_kernel, shares),
        out_shape=jax.ShapeDtypeStruct((rows, width), bf16),
        in_specs=[VMEM] * (4 + 2 * shares) + [any_space] * shares,
        out_specs=VMEM,
        scratch_shapes=[
            pltpu.VMEM((shares, *shape), bf16)
            for shape in ((2 * cols, width), (width, wide), (wide, width))
        ]
        + [pltpu.SemaphoreType.DMA((3, shares))],
        name="final",
        compiler_params=PARAMS,
        cost_estimate=pl.CostEstimate(
            flops=2 * rows * width * 4096, bytes_accessed=6 << 20, transcendentals=1 << 18
        ),
    )(share, gain, local, degree, *att, *far_sums, *bundles)


def gather_pieces(piece, axis):
    count = lax.axis_size(axis)
    pieces = {0: piece}
    bit = count // 2
    while bit:
        for k in list(pieces):
            pieces[k | bit] = lax.ppermute(pieces[k], axis, xor_route(count, bit))
        bit //= 2
    return [pieces[k] for k in range(count)]


def layer(
    x,
    mixer_gain,
    perceptron_gain,
    projectors,
    scale,
    out_projector,
    neighbour_projector,
    expand,
    contract,
    companion,
    sender,
    tally,
    landing,
    tail,
    sink,
):
    peers = lax.axis_size("dom")
    shares = lax.axis_size("mp")
    cols = projectors.shape[2]

    def send(block, mask):
        return lax.ppermute(block, "dom", xor_route(peers, mask))

    (
        low_mask, high_mask, pair, q, kv, k, v, bundle, scales, share, late_gain, landing,
        outgoing,
    ) = prologue(
        tally, companion, scale, x, mixer_gain[None, :], projectors, sender[0],
        (expand, contract, out_projector, neighbour_projector), perceptron_gain[None, :],
        landing[0], shares,
    )
    bundles = gather_pieces(bundle, "mp")
    nodes = x.shape[0]

    def beside(outgoing, tail, sink, x, most=EDGE_STEP):
        arrived = lax.all_to_all(outgoing, "dom", split_axis=0, concat_axis=0, tiled=True)
        return arrived, *edge_sums(tail, sink, x, nodes // shares, most)

    operands = (kv, k, v, outgoing, tail, sink, x)
    if peers * (peers - 1) // 2 <= 32:
        branches = []
        for high in range(1, peers):
            for low in range(1, high):

                def branch(kv, k, v, *rest, low=low, high=high):
                    most = EDGE_STEP
                    if low & high & (peers // 2):
                        most = EDGE_STEP_ON_PATH
                        one_k, one_v = send(k, low), send(v, low)
                        two_k, two_v = send(one_k, low ^ high), send(one_v, low ^ high)
                        one = jnp.concatenate([one_k, one_v], axis=1)
                        two = jnp.concatenate([two_k, two_v], axis=1)
                    else:
                        one, two = send(kv, low), send(kv, high)
                    return one, two, *beside(*rest, most)

                branches.append(branch)
        one, two, arrived, local, edge_degree = lax.switch(pair[0], branches, *operands)
    else:
        hops = [lambda kv, mask=mask: send(kv, mask) for mask in range(1, peers)]
        one = lax.switch(low_mask[0], hops, kv)
        two = lax.switch(high_mask[0], hops, kv)
        arrived, local, edge_degree = beside(outgoing, tail, sink, x)

    degree, *far_sums = landed_sums(edge_degree, landing, arrived, nodes, cols, shares)

    def swap(chunk, k):
        return lax.ppermute(chunk, "mp", xor_route(shares, k)) if k else chunk

    far_sums = [swap(chunk, k) for k, chunk in enumerate(far_sums)]
    groups = [tuple(range(shares // 2, shares)), tuple(range(shares // 2))]
    att = [None] * shares
    for group in groups:
        chunks = attention(scales, q, kv, one, two, shares, group)
        for k, chunk in zip(group, chunks):
            att[k] = swap(chunk, k)
    return final(share, late_gain, local, degree, att, far_sums, bundles)


def solution(mesh):
    return jax.shard_map(
        layer,
        mesh=mesh,
        in_specs=(
            P("dom", None),
            P(),
            P(),
            P(None, None, "mp"),
            P("mp"),
            P("mp", None),
            P("mp", None),
            P(None, "mp"),
            P("mp", None),
            P(),
            P("dom", None, None),
            P("dom", None),
            P("dom", None, None),
            P("dom", None),
            P("dom", None),
        ),
        out_specs=P(("dom", "mp"), None),
        check_vma=False,
    )
```
